512 devices in a mesh: tx: 32 (over y, x, core), ty: 16 (over z).
Axes of the slice: x: 4, y: 4, z: 16, core: 2. Of those that a mesh axis runs over, the one named last changes fastest.
Arguments:
- points: float32 [3, 1048576], P(None, ('tx', 'ty')), may hold values from 0 to 1
- tree_order: int32 [512, 2048], P(('tx', 'ty')), may hold values from 0 to 2047, each once within a row
- samples: float32 [1048576, 128], P(('tx', 'ty')), may hold values from -6 to 6
- near_leaves: int32 [4096, 5], P(('tx', 'ty')), may hold values from 0 to 11, as said below
- near_counts: int32 [4096], P(('tx', 'ty')), may hold values from 0 to 5, as said below
Outputs:
- leaf_bases: float32 [1048576, 128], P(('tx', 'ty'))
- local_bases: float32 [3584, 256, 128], P(('tx', 'ty'))
- upper_bases: float32 [4608, 256, 128], P(('tx', 'ty'))
- root_factor: float32 [128, 128], replicated
The draws below stay inside these ranges and needn't reach their ends.
Inputs may be any that keep to these rules, and one draw needn't show every extreme that they name: `near_leaves`: for k < near_counts[i], the entry w at [i, k] names the existing leaf (i // 8) * 8 - 2 + w, which is not i; the leaves named in one row are distinct; entries at k >= near_counts[i] are 0. `near_counts`: leaf 0 lists exactly 5 near-field leaves in every draw. `tree_order`: each row is a permutation of the positions of one device's block.
All inputs are finite; a program needn't handle non-finite values.
Results may differ from the reference program's by a relative error of at most 0.0003.
Values sent between devices are 32-bit elements; how exact they have to be, the bound alone decides.
No kernel may reach another device: no remote copies, remote signals or barrier semaphores. Data moves between devices by JAX's collectives and lax.ppermute only.
A program may use at most 64 MiB of HBM per device.

```python
import jax
import jax.numpy as jnp
from jax import lax

RANK = 128
LEAF = 256
LEAVES_DEV = 8
HALO = 2
MAXNB = 5
PTS_DEV = 2048
LEAVES = 4096
NPTS = 1048576
LEVELS = 9
DEVICES = 512


def near_lists(key):
    count_key, order_key = jax.random.split(jax.random.fold_in(key, 7))
    counts = jax.random.randint(count_key, (LEAVES,), 0, MAXNB + 1)
    counts = counts.at[0].set(MAXNB)
    window_width = LEAVES_DEV + 2 * HALO
    leaf_ids = jnp.arange(LEAVES, dtype=jnp.int32)
    device_ids = leaf_ids // LEAVES_DEV
    window = jnp.arange(window_width, dtype=jnp.int32)
    global_ids = device_ids[:, None] * LEAVES_DEV - HALO + window[None, :]
    invalid = (global_ids < 0) | (global_ids >= LEAVES) | (global_ids == leaf_ids[:, None])
    row_keys = jax.random.split(order_key, LEAVES)
    shuffled = jax.vmap(lambda row_key: jax.random.permutation(row_key, window_width))(row_keys)
    scores = shuffled.astype(jnp.int32) + window_width * invalid.astype(jnp.int32)
    chosen = jnp.argsort(scores, axis=1)[:, :MAXNB].astype(jnp.int32)
    filled = jnp.arange(MAXNB, dtype=jnp.int32)[None, :] < counts[:, None]
    return (jnp.where(filled, chosen, 0).astype(jnp.int32), counts.astype(jnp.int32))


def draw_near_leaves(key, part):
    return near_lists(key)[0]


def draw_near_counts(key, part):
    return near_lists(key)[1]


def block_scale(own_key, dims, cuts, low, top_value):
    factor_of, own = 1.0, jax.random.fold_in(own_key, 6)
    for dim, parts in cuts:
        draws = jnp.exp(jax.random.uniform(jax.random.fold_in(own, dim), (parts,), jnp.float32, low / len(cuts), top_value / len(cuts)))
        factor_of = factor_of * jnp.repeat(draws, dims[dim] // parts).reshape([-1 if axis == dim else 1 for axis in range(len(dims))])
    return factor_of


def normal_values(key, shape, deviation, limit, pieces=(), kind=jnp.bfloat16):
    factor_of = block_scale(key, shape, pieces, -0.22, 0.18) if pieces else 1.0
    array = jax.random.normal(key, shape, jnp.float32) * deviation * factor_of
    return jnp.minimum(jnp.maximum(array, -limit), limit).astype(kind)


def setup_inputs(seed: int = 0) -> dict:
    splits = jax.random.split(jax.random.key(seed), 6)
    points = jnp.clip(1.0 * jax.random.uniform(splits[0], (3, NPTS), jnp.float32) ** block_scale(splits[0], (3, NPTS), ((1, 512),), -0.2, 0.2), 0.0, 1.0)
    tree_order = jax.vmap(lambda own: jax.random.permutation(own, PTS_DEV))(jax.random.split(splits[1], DEVICES)).reshape((DEVICES, PTS_DEV)).astype(jnp.int32)
    samples = normal_values(splits[2], (NPTS, RANK), 1.0, 6.0, ((0, 512),), jnp.float32)
    near_leaves = draw_near_leaves(jax.random.fold_in(splits[5], 71), 0)
    near_counts = draw_near_counts(jax.random.fold_in(splits[5], 71), 0)
    return {"points": points, "tree_order": tree_order, "samples": samples, "near_leaves": near_leaves, "near_counts": near_counts}


SPREAD = 50.0

def orthonormalize(stacked):
    gram_matrix = jnp.einsum('...ir,...is->...rs', stacked, stacked, precision=lax.Precision.HIGHEST)
    lower_factor = jnp.linalg.cholesky(gram_matrix)
    basis_rows = jax.scipy.linalg.solve_triangular(lower_factor, jnp.swapaxes(stacked, -1, -2), lower=True)
    return (jnp.swapaxes(basis_rows, -1, -2), jnp.swapaxes(lower_factor, -1, -2))

def kernel_tile(row_points, column_points, column_samples, weight):
    distance = (row_points[0][:, :, None] - column_points[0][:, None, :]) ** 2
    for coord_index in range(1, 3):
        distance = distance + (row_points[coord_index][:, :, None] - column_points[coord_index][:, None, :]) ** 2
    kernel = jnp.exp(-SPREAD * distance) * weight[:, None, None]
    return jnp.einsum('lij,ljr->lir', kernel, column_samples, precision=lax.Precision.HIGHEST)

def reference(points, tree_order, samples, near_leaves, near_counts):
    ordered = jnp.take_along_axis(points.reshape(3, DEVICES, PTS_DEV), tree_order[None], axis=2)
    leaf_points = ordered.reshape(3, LEAVES, LEAF)
    leaf_samples = samples.reshape(LEAVES, LEAF, RANK)

    def device_section(device):
        first = device * LEAVES_DEV
        own_points = lax.dynamic_slice_in_dim(leaf_points, first, LEAVES_DEV, 1)
        own_samples = lax.dynamic_slice_in_dim(leaf_samples, first, LEAVES_DEV, 0)
        lists = lax.dynamic_slice_in_dim(near_leaves, first, LEAVES_DEV, 0)
        counts = lax.dynamic_slice_in_dim(near_counts, first, LEAVES_DEV, 0)
        sampled = kernel_tile(own_points, own_points, own_samples, jnp.ones((LEAVES_DEV,), jnp.float32))
        for position in range(MAXNB):
            column_leaf = jnp.clip(first - HALO + lists[:, position], 0, LEAVES - 1).astype(jnp.int32)
            weight = (counts > position).astype(jnp.float32)
            sampled = sampled + kernel_tile(own_points, leaf_points[:, column_leaf], leaf_samples[column_leaf], weight)
        return orthonormalize(sampled)
    leaf_basis, leaf_factor = lax.map(device_section, jnp.arange(DEVICES, dtype=jnp.int32))
    factors = leaf_factor.reshape(LEAVES, RANK, RANK)
    local_levels = []
    while factors.shape[0] > DEVICES:
        basis, factors = orthonormalize(factors.reshape(factors.shape[0] // 2, 2 * RANK, RANK))
        local_levels.append(basis.reshape(DEVICES, -1, 2 * RANK, RANK))
    local_bases = jnp.concatenate(local_levels, axis=1).reshape(DEVICES * (LEAVES_DEV - 1), 2 * RANK, RANK)
    upper_levels = []
    height = 0
    while factors.shape[0] > 1:
        basis, factors = orthonormalize(factors.reshape(factors.shape[0] // 2, 2 * RANK, RANK))
        height = height + 1
        upper_levels.append(jnp.repeat(basis, 2 ** height, axis=0))
    upper_bases = jnp.stack(upper_levels, axis=1).reshape(DEVICES * LEVELS, 2 * RANK, RANK)
    return (leaf_basis.reshape(NPTS, RANK), local_bases, upper_bases, factors[0])
```

```python
import jax
import jax.numpy as jnp
from jax import lax
from jax.experimental import pallas as pl
from jax.experimental.pallas import tpu as pltpu
from jax.sharding import PartitionSpec as P

HALO = 2
SPREAD = 50.0
F32 = jnp.float32
BF16 = jnp.bfloat16
BLK = 8
PARAMS = dict(vmem_limit_bytes=56 << 20)


def passed_along(block, axis, distance):
    devices = range(lax.axis_size(axis))
    route = [(i - distance, i) for i in devices if i - distance in devices]
    return lax.ppermute(block, axis, route)


def from_partner(value, axis, stride):
    mask = 2**stride
    pairs = [(source, source ^ mask) for source in range(lax.axis_size(axis))]
    return lax.ppermute(value, axis, pairs)


def pieces(x):
    a = x.astype(BF16).astype(F32)
    y = x - a
    b = y.astype(BF16).astype(F32)
    return a, b, y - b


def row_of(x, j):
    return jnp.broadcast_to(x[j : j + 1, :], x.shape)


def factor_groups(work, groups):
    lane = lax.broadcasted_iota(jnp.int32, (BLK, 128), 1)
    sub = lax.broadcasted_iota(jnp.int32, (BLK, 128), 0)
    for k in range(128 // BLK):
        r = BLK * k
        for group in groups:
            rows_a = {m: work[m, r : r + BLK, :128] for m in group}
            rows_i = {m: work[m, r : r + BLK, 128:] for m in group}
            diag = None
            for s, m in enumerate(group):
                shift = (BLK * s - r) % 128
                x = pltpu.roll(rows_a[m], shift, 1) if shift else rows_a[m]
                diag = x if s == 0 else jnp.where((lane >= BLK * s) & (lane < BLK * (s + 1)), x, diag)
            cols = [pltpu.roll(diag, 128 - j, 1) if j else diag for j in range(BLK)]
            inv = [jnp.where(sub == j, 1.0, 0.0).astype(F32) for j in range(BLK)]
            scale = jnp.ones((BLK, 128), F32)
            for j in range(BLK):
                rs = lax.rsqrt(row_of(cols[j], j))
                mult = jnp.where(sub > j, cols[j] * (rs * rs), 0.0)
                for q in range(j + 1, BLK):
                    cols[q] = cols[q] - mult * row_of(cols[q], j)
                for q in range(j + 1):
                    inv[q] = inv[q] - mult * row_of(inv[q], j)
                scale = jnp.where(sub == j, rs, scale)
            inv = [e * scale for e in inv]
            for s, m in enumerate(group):
                a = i = None
                for q in range(BLK):
                    x = jnp.broadcast_to(inv[q][:, BLK * s : BLK * s + 1], (BLK, 128))
                    ta = x * row_of(rows_a[m], q)
                    ti = x * row_of(rows_i[m], q)
                    a = ta if a is None else a + ta
                    i = ti if i is None else i + ti
                a = jnp.where(lane >= r + sub, a, 0.0)
                work[m, r : r + BLK, :128] = a
                work[m, r : r + BLK, 128:] = i
                if k < 128 // BLK - 1:
                    p1, p2, p3 = pieces(jnp.concatenate([a, i], axis=1))
                    rhs = jnp.concatenate([p1, p2, p1, p2, p3, p1], axis=0).astype(BF16)
                    lhs = jnp.concatenate([p1, p1, p2, p2, p1, p3], axis=0)[:, :128]
                    lhs = lhs.T[r + BLK :].astype(BF16)
                    update = lax.dot_general(lhs, rhs, (((1,), (0,)), ((), ())), preferred_element_type=F32)
                    work[m, r + BLK :, :] = work[m, r + BLK :, :] - update


def times_transposed(x, y):
    return lax.dot_general(
        x, y, (((1,), (1,)), ((), ())), precision=lax.Precision.HIGHEST, preferred_element_type=F32
    )


def identity():
    i = lax.broadcasted_iota(jnp.int32, (128, 128), 0)
    j = lax.broadcasted_iota(jnp.int32, (128, 128), 1)
    return (i == j).astype(F32)


def sample_kernel(
    near, counts, own_points, before_points, after_points, own, before, after, y_ref, g_ref, points, parts
):
    leaves = counts.shape[0]
    for w in range(leaves + 2 * HALO):
        if w < HALO:
            p, s, at = before_points, before, w
        elif w < leaves + HALO:
            p, s, at = own_points, own, w - HALO
        else:
            p, s, at = after_points, after, w - HALO - leaves
        points[w, 0:3, :] = p[:, at * 256 : at * 256 + 256]
        block = s[at * 256 : at * 256 + 256, :]
        high = block.astype(BF16)
        parts[w, :, :128] = high
        parts[w, :, 128:] = (block - high.astype(F32)).astype(BF16)

    def leaf(i, carry):
        rows = points[HALO + i].T

        def tile(w):
            cols = points[w]
            d = None
            for t in range(3):
                e = (rows[:, t : t + 1] - cols[t : t + 1, :]) ** 2
                d = e if d is None else d + e
            kernel = jnp.exp(-SPREAD * d)
            high = kernel.astype(BF16)
            low = (kernel - high.astype(F32)).astype(BF16)
            both = parts[w]
            out = jnp.dot(high, both, preferred_element_type=F32) + jnp.dot(
                low, both, preferred_element_type=F32
            )
            return out[:, :128] + out[:, 128:]

        y_ref[i] = tile(HALO + i)

        def near_one(k, c):
            y_ref[i] = y_ref[i] + tile(near[i, k])
            return c

        lax.fori_loop(0, counts[i], near_one, 0)
        y = y_ref[i]
        g_ref[i] = lax.dot_general(
            y, y, (((0,), (0,)), ((), ())), precision=lax.Precision.HIGHEST, preferred_element_type=F32
        )
        return carry

    lax.fori_loop(0, leaves, leaf, 0)
    at = 0
    n = leaves
    while n > 1:
        for c in range(n // 2):
            g_ref[at + n + c] = g_ref[at + 2 * c] + g_ref[at + 2 * c + 1]
        at += n
        n //= 2


def local_kernel(g_ref, y_ref, leaf_ref, base_ref, root_ref, work):
    total = g_ref.shape[0]
    leaves = (total + 1) // 2
    eye = identity()
    for m in range(total):
        work[m, :, :128] = g_ref[m]
        work[m, :, 128:] = eye
    factor_groups(work, [list(range(total))])
    for m in range(leaves):
        leaf_ref[m * 256 : m * 256 + 256, :] = times_transposed(y_ref[m], work[m, :, 128:])
    for n in range(leaves, total):
        c = 2 * (n - leaves)
        for half in range(2):
            base_ref[n - leaves, half * 128 : half * 128 + 128, :] = times_transposed(
                work[c + half, :, :128], work[n, :, 128:]
            )
    root_ref[...] = work[total - 1, :, :128]


def upper_kernel(flags, root_in, own_ref, partner_ref, base_ref, root_ref, work):
    levels = own_ref.shape[0]
    eye = identity()
    for m in range(levels):
        work[m, :, :128] = own_ref[m]
        work[m, :, 128:] = eye
        work[levels + m, :, :128] = partner_ref[m]
        work[levels + m, :, 128:] = eye
    factor_groups(work, [list(range(levels)), list(range(levels, 2 * levels))])
    for h in range(levels):
        mine = root_in[...] if h == 0 else work[h - 1, :, :128]
        other = work[levels + h, :, :128]
        inverse = work[h, :, 128:]
        a = times_transposed(mine, inverse)
        b = times_transposed(other, inverse)
        upper = flags[h] == 1
        base_ref[h, :128, :] = jnp.where(upper, b, a)
        base_ref[h, 128:, :] = jnp.where(upper, a, b)
    root_ref[...] = work[levels - 1, :, :128]


def call(kernel, outs, scratch, prefetch, args):
    vmem = pl.BlockSpec(memory_space=pltpu.VMEM)
    smem = pl.BlockSpec(memory_space=pltpu.SMEM)
    return pl.pallas_call(
        kernel,
        out_shape=tuple(jax.ShapeDtypeStruct(s, F32) for s in outs),
        in_specs=[smem] * prefetch + [vmem] * (len(args) - prefetch),
        out_specs=tuple([vmem] * len(outs)),
        scratch_shapes=scratch,
        compiler_params=pltpu.CompilerParams(**PARAMS),
    )(*args)


def per_device(points, tree_order, samples, near_leaves, near_counts):
    leaves = near_counts.shape[0]
    both = ("tx", "ty")
    edge = HALO * 256
    before = passed_along(samples[-edge:], both, 1)
    after = passed_along(samples[:edge], both, -1)
    ordered = jnp.take(points, tree_order[0], axis=1)
    before_points = passed_along(ordered[:, -edge:], both, 1)
    after_points = passed_along(ordered[:, :edge], both, -1)
    window = leaves + 2 * HALO
    nodes = 2 * leaves - 1
    sampled, grams = call(
        sample_kernel,
        [(leaves, 256, 128), (nodes, 128, 128)],
        [pltpu.VMEM((window, 8, 256), F32), pltpu.VMEM((window, 256, 256), BF16)],
        2,
        (near_leaves, near_counts, ordered, before_points, after_points, samples, before, after),
    )
    gram = grams[nodes - 1]
    owns, partners, flags = [], [], []
    for axis in ("ty", "tx"):
        for height in range(lax.axis_size(axis).bit_length() - 1):
            partner = from_partner(gram, axis, height)
            gram = gram + partner
            owns.append(gram)
            partners.append(partner)
            flags.append(lax.axis_index(axis) // 2**height % 2)
    leaf_bases, local_bases, local_root = call(
        local_kernel,
        [(leaves * 256, 128), (leaves - 1, 256, 128), (128, 128)],
        [pltpu.VMEM((nodes, 128, 256), F32)],
        0,
        (grams, sampled),
    )
    levels = len(owns)
    upper_bases, root = call(
        upper_kernel,
        [(levels, 256, 128), (128, 128)],
        [pltpu.VMEM((2 * levels, 128, 256), F32)],
        1,
        (jnp.stack(flags), local_root, jnp.stack(owns), jnp.stack(partners)),
    )
    return leaf_bases, local_bases, upper_bases, root


def solution(mesh):
    return jax.shard_map(
        per_device,
        mesh=mesh,
        in_specs=(
            P(None, ("tx", "ty")),
            P(("tx", "ty"), None),
            P(("tx", "ty"), None),
            P(("tx", "ty"), None),
            P(("tx", "ty")),
        ),
        out_specs=(
            P(("tx", "ty"), None),
            P(("tx", "ty"), None, None),
            P(("tx", "ty"), None, None),
            P(),
        ),
        check_vma=False,
    )
```

```python
import jax
import jax.numpy as jnp
from jax import lax
from jax.experimental import pallas as pl
from jax.experimental.pallas import tpu as pltpu
from jax.sharding import PartitionSpec as P

F32 = jnp.float32
BF16 = jnp.bfloat16
HALO = 2
SPREAD = 50.0
LOG2E = 1.4426950408889634
EXTRA = 64
BLK = 8

def pieces(x):
    a=x.astype(BF16).astype(F32); y=x-a
    b=y.astype(BF16).astype(F32)
    return a,b,y-b
def call(kernel, outs, scratch, prefetch, args, specs=None, alias=None):
    vmem = pl.BlockSpec(memory_space=pltpu.VMEM)
    smem = pl.BlockSpec(memory_space=pltpu.SMEM)
    return pl.pallas_call(kernel,
        out_shape=tuple(jax.ShapeDtypeStruct(s, F32) for s in outs),
        in_specs=[smem] * prefetch + (specs or [vmem] * (len(args) - prefetch)),
        out_specs=tuple([vmem] * len(outs)),
        scratch_shapes=scratch, input_output_aliases=alias or {},
        compiler_params=pltpu.CompilerParams(vmem_limit_bytes=56<<20))(*args)

def edge_kernel(first, last, points, order, up, down):
    n = first.shape[0]
    for out, rows, at in ((up, last, order.shape[1] - n), (down, first, 0)):
        out[:n, :] = rows[...]
        for c in range(3):
            for h in range(16):
                out[n + 16 * c + h : n + 16 * c + h + 1, :] = points[c : c + 1, 128 * h : 128 * h + 128]
        for h in range(n // 128):
            out[n + 48 + h : n + 49 + h, :] = order[:, at + 128 * h : at + 128 * h + 128].astype(F32)
        out[n + 48 + n // 128 :, :] = jnp.zeros((16 - n // 128, 128), F32)

def table_of(rows48):
    return jnp.concatenate(pieces(rows48), axis=0).astype(BF16)

def gathered(table, order_row):
    low = order_row & 127
    high = order_row >> 7
    hot = (lax.broadcasted_iota(jnp.int32, (128, 128), 0) == low).astype(F32).astype(BF16)
    r = jnp.dot(table, hot, preferred_element_type=F32)
    r = (r[0:48] + r[48:96]) + r[96:144]
    pick = lax.broadcasted_iota(jnp.int32, (16, 128), 0) == high
    return [jnp.sum(jnp.where(pick, r[16 * c : 16 * c + 16], 0.0), axis=0, keepdims=True) for c in range(3)]

def split_into(parts, w, block):
    high = block.astype(BF16)
    parts[w, :, :128] = high
    parts[w, :, 128:] = (block - high.astype(F32)).astype(BF16)

def spread_rows(points, rows, i):
    t = points[i].T
    for c in range(3):
        rows[i, c] = jnp.broadcast_to(t[:, c : c + 1], (256, 128))

def tile(rows, i, points, parts, w):
    cols = points[w]
    halves = []
    for g in range(2):
        d = None
        for c in range(3):
            e = rows[i, c] - cols[c : c + 1, 128 * g : 128 * g + 128]
            d = e * e if d is None else d + e * e
        halves.append(jnp.exp2(d * (-SPREAD * LOG2E)))
    kernel = jnp.concatenate(halves, axis=1)
    high = kernel.astype(BF16)
    low = (kernel - high.astype(F32)).astype(BF16)
    both = parts[w]
    out = jnp.dot(high, both, preferred_element_type=F32) + jnp.dot(low, both, preferred_element_type=F32)
    return out[:, :128] + out[:, 128:]

def list_tiles(near, counts, leaf_of, col_of, wanted, start):
    leaves = counts.shape[0]
    def leaf(i, n):
        def one(k, n):
            w = near[i, k]
            leaf_of[n] = i
            col_of[n] = w
            return n + jnp.where(wanted(w), 1, 0).astype(jnp.int32)
        return lax.fori_loop(0, counts[i], one, n)
    n = lax.fori_loop(0, leaves, leaf, start)
    return n

def run_tiles(n, leaf_of, col_of, at, y, spare, rows, points, parts, width=2):
    leaf_of_pad = spare
    for e in range(width):
        leaf_of[n + e] = spare
        col_of[n + e] = at
    def step(s, c):
        ids = [(leaf_of[s * width + e], col_of[s * width + e] - at) for e in range(width)]
        outs = [tile(rows, jnp.minimum(i, spare - 1), points, parts, w) for i, w in ids]
        for (i, _), o in zip(ids, outs):
            y[i] = y[i] + o
        return c
    lax.fori_loop(0, (n + width - 1) // width, step, 0)

def own_kernel(near, counts, raw, order, own, y_ref, p_ref, acc, parts, rows, tab, leaf_of, col_of):
    leaves = counts.shape[0]
    for c in range(3):
        for h in range(16):
            tab[16 * c + h : 16 * c + h + 1, :] = raw[c : c + 1, 128 * h : 128 * h + 128]
    table = table_of(tab[...])
    for h in range(2 * leaves):
        got = gathered(table, order[:, 128 * h : 128 * h + 128])
        for c in range(3):
            p_ref[h // 2, c : c + 1, 128 * (h % 2) : 128 * (h % 2) + 128] = got[c]
    for i in range(leaves):
        split_into(parts, i, own[256 * i : 256 * i + 256, :])
        p_ref[i, 3:8, :] = jnp.zeros((5, 256), F32)
        spread_rows(p_ref, rows, i)
        leaf_of[i] = i
        col_of[i] = HALO + i
        acc[i] = jnp.zeros((256, 128), F32)
    acc[leaves] = jnp.zeros((256, 128), F32)
    n = list_tiles(near, counts, leaf_of, col_of, lambda w: (w >= HALO) & (w < HALO + leaves), leaves)
    run_tiles(n, leaf_of, col_of, HALO, acc, leaves, rows, p_ref, parts)
    y_ref[...] = acc[:leaves]

def halo_kernel(near, counts, before, after, y_in, p_in, y_ref, g_ref, acc, parts, rows, points, leaf_of, col_of):
    leaves = counts.shape[0]
    n_edge = HALO * 256
    for side, src in ((0, before), (1, after)):
        table = table_of(src[n_edge : n_edge + 48, :])
        for h in range(2 * HALO):
            got = gathered(table, src[n_edge + 48 + h : n_edge + 49 + h, :].astype(jnp.int32))
            for c in range(3):
                points[side * HALO + h // 2, c : c + 1, 128 * (h % 2) : 128 * (h % 2) + 128] = got[c]
        for w in range(HALO):
            split_into(parts, side * HALO + w, src[256 * w : 256 * w + 256, :])
    for i in range(leaves):
        spread_rows(p_in, rows, i)
        acc[i] = y_in[i]
    acc[leaves] = jnp.zeros((256, 128), F32)
    n = list_tiles(near, counts, leaf_of, col_of, lambda w: (w < HALO) | (w >= HALO + leaves), 0)
    def fix(t, c):
        w = col_of[t]
        col_of[t] = jnp.where(w < HALO, w, w - leaves)
        return c
    lax.fori_loop(0, n, fix, 0)
    run_tiles(n, leaf_of, col_of, 0, acc, leaves, rows, points, parts)
    for i in range(leaves):
        y = acc[i]
        y_ref[i] = y
        b1, b2, b3 = [p.astype(BF16) for p in pieces(y)]
        b12 = jnp.concatenate([b1, b2], axis=1)
        q = jnp.dot(b12.T, b12, preferred_element_type=F32)
        q = (q[:128] + q[128:])
        t = jnp.dot(b1.T, b3, preferred_element_type=F32) + jnp.dot(b3.T, b1, preferred_element_type=F32)
        g_ref[i] = (q[:, :128] + q[:, 128:]) + t
    at, n = 0, leaves
    while n > 1:
        for c in range(n // 2):
            g_ref[at + n + c] = g_ref[at + 2 * c] + g_ref[at + 2 * c + 1]
        at += n
        n //= 2

def edge_blocks(points, order, samples):
    n = HALO * 256
    total = samples.shape[0] // n
    specs = [pl.BlockSpec((n, 128), lambda i: (0, 0)), pl.BlockSpec((n, 128), lambda i: (total - 1, 0)),
             pl.BlockSpec(points.shape, lambda i: (0, 0)), pl.BlockSpec(order.shape, lambda i: (0, 0))]
    o = pl.BlockSpec((n + EXTRA, 128), lambda i: (0, 0))
    return pl.pallas_call(edge_kernel, grid=(1,), in_specs=specs, out_specs=(o, o),
        out_shape=(jax.ShapeDtypeStruct((n + EXTRA, 128), F32),) * 2)(samples, samples, points, order)
def own_samples(near, counts, points, order, samples):
    L = counts.shape[0]
    return call(own_kernel, [(L,256,128),(L,8,256)],
        [pltpu.VMEM((L+1,256,128),F32), pltpu.VMEM((L,256,256),BF16), pltpu.VMEM((L,3,256,128),F32), pltpu.VMEM((48,128),F32), pltpu.SMEM((64,),jnp.int32), pltpu.SMEM((64,),jnp.int32)],
        2, (near, counts, points, order, samples))
def halo_samples(near, counts, before, after, y, p):
    L = counts.shape[0]
    return call(halo_kernel, [(L,256,128),(2*L-1,128,128)],
        [pltpu.VMEM((L+1,256,128),F32), pltpu.VMEM((2*HALO,256,256),BF16), pltpu.VMEM((L,3,256,128),F32), pltpu.VMEM((2*HALO,8,256),F32), pltpu.SMEM((64,),jnp.int32), pltpu.SMEM((64,),jnp.int32)],
        2, (near, counts, before, after, y, p))


def passed_along(block, axis, distance):
    devices = range(lax.axis_size(axis))
    route = [(i - distance, i) for i in devices if i - distance in devices]
    return lax.ppermute(block, axis, route)


def exchanged(value, axis, mask):
    return lax.ppermute(value, axis, [(i, i ^ mask) for i in range(lax.axis_size(axis))])


def row_of(x, j):
    return jnp.broadcast_to(x[j : j + 1, :], x.shape)


def factor_all(work, upper_out, inverse_out, groups):
    lane = lax.broadcasted_iota(jnp.int32, (BLK, 128), 1)
    sub = lax.broadcasted_iota(jnp.int32, (BLK, 128), 0)
    for k in range(128 // BLK):
        r = BLK * k
        on_diag = (lane >= r) & (lane < r + BLK)
        for group in groups:
            panel = {m: work[m, r : r + BLK, :] for m in group}
            diag = None
            for s, m in enumerate(group):
                shift = (BLK * s - r) % 128
                x = pltpu.roll(panel[m], shift, 1) if shift else panel[m]
                diag = x if s == 0 else jnp.where((lane >= BLK * s) & (lane < BLK * s + BLK), x, diag)
            cols = [pltpu.roll(diag, 128 - j, 1) if j else diag for j in range(BLK)]
            inv = [jnp.where(sub == j, 1.0, 0.0).astype(F32) for j in range(BLK)]
            scale = jnp.ones((BLK, 128), F32)
            for j in range(BLK):
                below = jnp.where(sub > j, cols[j], 0.0)
                rs = lax.rsqrt(row_of(cols[j], j))
                mult = below * rs
                for q in range(j + 1, BLK):
                    cols[q] = cols[q] - mult * (row_of(cols[q], j) * rs)
                for q in range(j + 1):
                    inv[q] = inv[q] - mult * (row_of(inv[q], j) * rs)
                scale = jnp.where(sub == j, rs, scale)
            inv = [e * scale for e in inv]
            for s, m in enumerate(group):
                out = block = None
                for q in range(BLK):
                    x = jnp.broadcast_to(inv[q][:, BLK * s : BLK * s + 1], (BLK, 128))
                    t = x * row_of(panel[m], q)
                    out = t if q == 0 else out + t
                    block = x if q == 0 else jnp.where(lane == r + q, x, block)
                upper_out[m, r : r + BLK, :] = jnp.where(lane >= r + sub, out, 0.0)
                right = jnp.where(on_diag, block, out)
                inverse_out[m, r : r + BLK, :] = jnp.where(lane < r + BLK, right, 0.0)
                if r + BLK < 128:
                    p1, p2, p3 = pieces(right)
                    rhs = jnp.concatenate([p1, p2, p1, p2, p3, p1], axis=0).astype(BF16)
                    lhs = jnp.concatenate([p1, p1, p2, p2, p1, p3], axis=0).astype(BF16)
                    update = jnp.dot(lhs.T[r + BLK :], rhs, preferred_element_type=F32)
                    at = lax.broadcasted_iota(jnp.int32, (128 - r - BLK, 128), 1)
                    old = work[m, r + BLK :, :]
                    work[m, r + BLK :, :] = jnp.where((at >= r) & (at < r + BLK), 0.0, old) - update


def times_transposed(x, y):
    return lax.dot_general(
        x, y, (((1,), (1,)), ((), ())), precision=lax.Precision.HIGHEST, preferred_element_type=F32
    )


def local_factor_kernel(g_ref, upper_ref, inverse_ref, work):
    work[...] = g_ref[...]
    factor_all(work, upper_ref, inverse_ref, [list(range(g_ref.shape[0]))])


def local_basis_kernel(y_ref, upper_ref, inverse_ref, leaf_ref, base_ref):
    leaves = y_ref.shape[0]
    for m in range(leaves):
        leaf_ref[m * 256 : m * 256 + 256, :] = times_transposed(y_ref[m], inverse_ref[m])
    for n in range(leaves - 1):
        for half in range(2):
            base_ref[n, half * 128 : half * 128 + 128, :] = times_transposed(
                upper_ref[2 * n + half], inverse_ref[leaves + n]
            )


def upper_kernel(low_bits, *refs):
    levels = (len(refs) - 6) // 2
    first = refs[0]
    own = refs[1 : 1 + levels]
    partner = refs[1 + levels : 1 + 2 * levels]
    base_ref, root_ref, work, upper, inverse = refs[1 + 2 * levels :]
    place = (lax.axis_index("tx") << low_bits) + lax.axis_index("ty")
    for m in range(levels):
        work[m] = own[m][...]
        work[levels + m] = partner[m][...]
    factor_all(work, upper, inverse, [list(range(levels)), list(range(levels, 2 * levels))])
    for h in range(levels):
        mine = first[...] if h == 0 else upper[h - 1]
        a = times_transposed(mine, inverse[h])
        b = times_transposed(upper[levels + h], inverse[h])
        bit = (place >> h) & 1
        base_ref[h, pl.ds(bit * 128, 128), :] = a
        base_ref[h, pl.ds((1 - bit) * 128, 128), :] = b
    root_ref[...] = upper[levels - 1]


def per_device(points, tree_order, samples, near_leaves, near_counts):
    leaves = near_counts.shape[0]
    nodes = 2 * leaves - 1
    both = ("tx", "ty")
    for_after, for_before = edge_blocks(points, tree_order, samples)
    before = passed_along(for_after, both, 1)
    after = passed_along(for_before, both, -1)
    part, ordered = own_samples(near_leaves, near_counts, points, tree_order, samples)
    sampled, grams = halo_samples(near_leaves, near_counts, before, after, part, ordered)
    gram = grams[nodes - 1]
    owns, partners = [], []
    low_bits = lax.axis_size("ty").bit_length() - 1
    high_bits = lax.axis_size("tx").bit_length() - 1
    steps = [("ty", m) for m in [1, 2, 4, 15]] + [("tx", m) for m in [1, 2, 6, 8, 24]]
    assert [m.bit_length() for _, m in steps] == [*range(1, low_bits + 1), *range(1, high_bits + 1)]
    for h, (axis, mask) in enumerate(steps):
        if h == 2:
            grams, gram = lax.optimization_barrier((grams, gram))
        if h == 3:
            sampled, gram = lax.optimization_barrier((sampled, gram))
        partner = exchanged(gram, axis, mask)
        if h == 2:
            uppers, inverses = call(
                local_factor_kernel, [(nodes, 128, 128)] * 2, [pltpu.VMEM((nodes, 128, 128), F32)], 0, (grams,)
            )
            partner, uppers, inverses = lax.optimization_barrier((partner, uppers, inverses))
        if h == 3:
            leaf_bases, local_bases = call(
                local_basis_kernel,
                [(leaves * 256, 128), (leaves - 1, 256, 128)],
                [],
                0,
                (sampled, uppers, inverses),
            )
            partner, leaf_bases, local_bases = lax.optimization_barrier((partner, leaf_bases, local_bases))
        gram = gram + partner
        owns.append(gram)
        partners.append(partner)
    levels = len(owns)
    upper_bases, root = call(
        lambda *refs: upper_kernel(low_bits, *refs),
        [(levels, 256, 128), (128, 128)],
        [pltpu.VMEM((2 * levels, 128, 128), F32)] * 3,
        0,
        (uppers[nodes - 1], *owns, *partners),
    )
    return leaf_bases, local_bases, upper_bases, root


def solution(mesh):
    return jax.shard_map(
        per_device,
        mesh=mesh,
        in_specs=(
            P(None, ("tx", "ty")),
            P(("tx", "ty"), None),
            P(("tx", "ty"), None),
            P(("tx", "ty"), None),
            P(("tx", "ty")),
        ),
        out_specs=(
            P(("tx", "ty"), None),
            P(("tx", "ty"), None, None),
            P(("tx", "ty"), None, None),
            P(),
        ),
        check_vma=False,
    )
```

```python
import jax
import jax.numpy as jnp
from jax import lax
from jax.experimental import pallas as pl
from jax.experimental.pallas import tpu as pltpu
from jax.sharding import PartitionSpec as P

F32 = jnp.float32
BF16 = jnp.bfloat16
HALO = 2
SPREAD = 50.0
LOG2E = 1.4426950408889634
EXTRA = 64
BLK = 8

def pieces(x):
    a=x.astype(BF16).astype(F32); y=x-a
    b=y.astype(BF16).astype(F32)
    return a,b,y-b
def call(kernel, outs, scratch, prefetch, args, specs=None, alias=None):
    vmem = pl.BlockSpec(memory_space=pltpu.VMEM)
    smem = pl.BlockSpec(memory_space=pltpu.SMEM)
    return pl.pallas_call(kernel,
        out_shape=tuple(jax.ShapeDtypeStruct(s, F32) for s in outs),
        in_specs=[smem] * prefetch + (specs or [vmem] * (len(args) - prefetch)),
        out_specs=tuple([vmem] * len(outs)),
        scratch_shapes=scratch, input_output_aliases=alias or {},
        compiler_params=pltpu.CompilerParams(vmem_limit_bytes=56<<20))(*args)

def edge_kernel(first, last, points, order, up, down):
    n = first.shape[0]
    for out, rows, at in ((up, last, order.shape[1] - n), (down, first, 0)):
        out[:n, :] = rows[...]
        for c in range(3):
            for h in range(16):
                out[n + 16 * c + h : n + 16 * c + h + 1, :] = points[c : c + 1, 128 * h : 128 * h + 128]
        for h in range(n // 128):
            out[n + 48 + h : n + 49 + h, :] = order[:, at + 128 * h : at + 128 * h + 128].astype(F32)
        out[n + 48 + n // 128 :, :] = jnp.zeros((16 - n // 128, 128), F32)

def table_of(rows48):
    return jnp.concatenate(pieces(rows48), axis=0).astype(BF16)

def gathered(table, order_row):
    low = order_row & 127
    high = order_row >> 7
    hot = (lax.broadcasted_iota(jnp.int32, (128, 128), 0) == low).astype(F32).astype(BF16)
    r = jnp.dot(table, hot, preferred_element_type=F32)
    r = (r[0:48] + r[48:96]) + r[96:144]
    pick = lax.broadcasted_iota(jnp.int32, (16, 128), 0) == high
    return [jnp.sum(jnp.where(pick, r[16 * c : 16 * c + 16], 0.0), axis=0, keepdims=True) for c in range(3)]

def split_into(parts, w, block):
    high = block.astype(BF16)
    parts[w, :, :128] = high
    parts[w, :, 128:] = (block - high.astype(F32)).astype(BF16)

def spread_rows(points, rows, i):
    t = points[i].T
    for c in range(3):
        rows[i, c] = jnp.broadcast_to(t[:, c : c + 1], (256, 128))

def tile(rows, i, points, parts, w):
    cols = points[w]
    halves = []
    for g in range(2):
        d = None
        for c in range(3):
            e = rows[i, c] - cols[c : c + 1, 128 * g : 128 * g + 128]
            d = e * e if d is None else d + e * e
        halves.append(jnp.exp2(d * (-SPREAD * LOG2E)))
    kernel = jnp.concatenate(halves, axis=1)
    high = kernel.astype(BF16)
    low = (kernel - high.astype(F32)).astype(BF16)
    both = parts[w]
    out = jnp.dot(high, both, preferred_element_type=F32) + jnp.dot(low, both, preferred_element_type=F32)
    return out[:, :128] + out[:, 128:]

def packed(g, out):
    lane = lax.broadcasted_iota(jnp.int32, (1, 128), 1)
    out[0:32, :] = g[0:32]
    out[32:64, :] = jnp.where(lane < 32, pltpu.roll(g[96:128], 32, 1), g[32:64])
    out[64:80, :] = jnp.where(lane < 64, pltpu.roll(g[80:96], 64, 1), g[64:80])


def unpacked(p, out, m):
    out[m, 0:64, :] = p[0:64, :]
    out[m, 64:80, :] = p[64:80, :]
    out[m, 80:96, :] = pltpu.roll(p[64:80, :], 64, 1)
    out[m, 96:128, :] = pltpu.roll(p[32:64, :], 96, 1)


def list_tiles(near, counts, leaf_of, col_of, wanted, start):
    leaves = counts.shape[0]
    def leaf(i, n):
        def one(k, n):
            w = near[i, k]
            leaf_of[n] = i
            col_of[n] = w
            return n + jnp.where(wanted(w), 1, 0).astype(jnp.int32)
        return lax.fori_loop(0, counts[i], one, n)
    n = lax.fori_loop(0, leaves, leaf, start)
    return n

def run_tiles(n, leaf_of, col_of, at, y, spare, rows, points, parts, width=2):
    leaf_of_pad = spare
    for e in range(width):
        leaf_of[n + e] = spare
        col_of[n + e] = at
    def step(s, c):
        ids = [(leaf_of[s * width + e], col_of[s * width + e] - at) for e in range(width)]
        outs = [tile(rows, jnp.minimum(i, spare - 1), points, parts, w) for i, w in ids]
        for (i, _), o in zip(ids, outs):
            y[i] = y[i] + o
        return c
    lax.fori_loop(0, (n + width - 1) // width, step, 0)

def own_kernel(near, counts, raw, order, own, y_ref, p_ref, acc, parts, rows, tab, leaf_of, col_of):
    leaves = counts.shape[0]
    for c in range(3):
        for h in range(16):
            tab[16 * c + h : 16 * c + h + 1, :] = raw[c : c + 1, 128 * h : 128 * h + 128]
    table = table_of(tab[...])
    for h in range(2 * leaves):
        got = gathered(table, order[:, 128 * h : 128 * h + 128])
        for c in range(3):
            p_ref[h // 2, c : c + 1, 128 * (h % 2) : 128 * (h % 2) + 128] = got[c]
    for i in range(leaves):
        split_into(parts, i, own[256 * i : 256 * i + 256, :])
        p_ref[i, 3:8, :] = jnp.zeros((5, 256), F32)
        spread_rows(p_ref, rows, i)
        leaf_of[i] = i
        col_of[i] = HALO + i
        acc[i] = jnp.zeros((256, 128), F32)
    acc[leaves] = jnp.zeros((256, 128), F32)
    n = list_tiles(near, counts, leaf_of, col_of, lambda w: (w >= HALO) & (w < HALO + leaves), leaves)
    run_tiles(n, leaf_of, col_of, HALO, acc, leaves, rows, p_ref, parts)
    y_ref[...] = acc[:leaves]

def halo_kernel(near, counts, before, after, y_in, p_in, y_ref, g_ref, top_ref, acc, parts, rows, points, leaf_of, col_of):
    leaves = counts.shape[0]
    n_edge = HALO * 256
    for side, src in ((0, before), (1, after)):
        table = table_of(src[n_edge : n_edge + 48, :])
        for h in range(2 * HALO):
            got = gathered(table, src[n_edge + 48 + h : n_edge + 49 + h, :].astype(jnp.int32))
            for c in range(3):
                points[side * HALO + h // 2, c : c + 1, 128 * (h % 2) : 128 * (h % 2) + 128] = got[c]
        for w in range(HALO):
            split_into(parts, side * HALO + w, src[256 * w : 256 * w + 256, :])
    for i in range(leaves):
        spread_rows(p_in, rows, i)
        acc[i] = y_in[i]
    acc[leaves] = jnp.zeros((256, 128), F32)
    n = list_tiles(near, counts, leaf_of, col_of, lambda w: (w < HALO) | (w >= HALO + leaves), 0)
    def fix(t, c):
        w = col_of[t]
        col_of[t] = jnp.where(w < HALO, w, w - leaves)
        return c
    lax.fori_loop(0, n, fix, 0)
    run_tiles(n, leaf_of, col_of, 0, acc, leaves, rows, points, parts)
    for i in range(leaves):
        y = acc[i]
        y_ref[i] = y
        b1, b2, b3 = [p.astype(BF16) for p in pieces(y)]
        b12 = jnp.concatenate([b1, b2], axis=1)
        q = jnp.dot(b12.T, b12, preferred_element_type=F32)
        q = (q[:128] + q[128:])
        t = jnp.dot(b1.T, b3, preferred_element_type=F32) + jnp.dot(b3.T, b1, preferred_element_type=F32)
        g_ref[i] = (q[:, :128] + q[:, 128:]) + t
    at, n = 0, leaves
    while n > 1:
        for c in range(n // 2):
            g_ref[at + n + c] = g_ref[at + 2 * c] + g_ref[at + 2 * c + 1]
        at += n
        n //= 2
    packed(g_ref[at], top_ref)

def edge_blocks(points, order, samples):
    n = HALO * 256
    total = samples.shape[0] // n
    specs = [pl.BlockSpec((n, 128), lambda i: (0, 0)), pl.BlockSpec((n, 128), lambda i: (total - 1, 0)),
             pl.BlockSpec(points.shape, lambda i: (0, 0)), pl.BlockSpec(order.shape, lambda i: (0, 0))]
    o = pl.BlockSpec((n + EXTRA, 128), lambda i: (0, 0))
    return pl.pallas_call(edge_kernel, grid=(1,), in_specs=specs, out_specs=(o, o),
        out_shape=(jax.ShapeDtypeStruct((n + EXTRA, 128), F32),) * 2)(samples, samples, points, order)
def own_samples(near, counts, points, order, samples):
    L = counts.shape[0]
    return call(own_kernel, [(L,256,128),(L,8,256)],
        [pltpu.VMEM((L+1,256,128),F32), pltpu.VMEM((L,256,256),BF16), pltpu.VMEM((L,3,256,128),F32), pltpu.VMEM((48,128),F32), pltpu.SMEM((64,),jnp.int32), pltpu.SMEM((64,),jnp.int32)],
        2, (near, counts, points, order, samples))
def halo_samples(near, counts, before, after, y, p):
    L = counts.shape[0]
    return call(halo_kernel, [(L,256,128),(2*L-1,128,128),(80,128)],
        [pltpu.VMEM((L+1,256,128),F32), pltpu.VMEM((2*HALO,256,256),BF16), pltpu.VMEM((L,3,256,128),F32), pltpu.VMEM((2*HALO,8,256),F32), pltpu.SMEM((64,),jnp.int32), pltpu.SMEM((64,),jnp.int32)],
        2, (near, counts, before, after, y, p))


def passed_along(block, axis, distance):
    devices = range(lax.axis_size(axis))
    route = [(i - distance, i) for i in devices if i - distance in devices]
    return lax.ppermute(block, axis, route)


def exchanged(value, axis, mask):
    return lax.ppermute(value, axis, [(i, i ^ mask) for i in range(lax.axis_size(axis))])


def row_of(x, j):
    return jnp.broadcast_to(x[j : j + 1, :], x.shape)


def factor_blocks(work, upper_out, inverse_out, groups, first=0, last=128 // BLK):
    base = BLK * first
    lane = lax.broadcasted_iota(jnp.int32, (BLK, 128), 1)
    sub = lax.broadcasted_iota(jnp.int32, (BLK, 128), 0)
    for k in range(first, last):
        r = BLK * k
        on_diag = (lane >= r) & (lane < r + BLK)
        for group in groups:
            panel = {m: work[m, r - base : r + BLK - base, :] for m in group}
            diag = None
            for s, m in enumerate(group):
                shift = (BLK * s - r) % 128
                x = pltpu.roll(panel[m], shift, 1) if shift else panel[m]
                diag = x if s == 0 else jnp.where((lane >= BLK * s) & (lane < BLK * s + BLK), x, diag)
            cols = [pltpu.roll(diag, 128 - j, 1) if j else diag for j in range(BLK)]
            inv = [jnp.where(sub == j, 1.0, 0.0).astype(F32) for j in range(BLK)]
            scale = jnp.ones((BLK, 128), F32)
            for j in range(BLK):
                below = jnp.where(sub > j, cols[j], 0.0)
                rs = lax.rsqrt(row_of(cols[j], j))
                mult = below * rs
                for q in range(j + 1, BLK):
                    cols[q] = cols[q] - mult * (row_of(cols[q], j) * rs)
                for q in range(j + 1):
                    inv[q] = inv[q] - mult * (row_of(inv[q], j) * rs)
                scale = jnp.where(sub == j, rs, scale)
            inv = [e * scale for e in inv]
            for s, m in enumerate(group):
                block, terms = None, []
                for q in range(BLK):
                    x = jnp.broadcast_to(inv[q][:, BLK * s : BLK * s + 1], (BLK, 128))
                    terms.append(x * row_of(panel[m], q))
                    block = x if q == 0 else jnp.where(lane == r + q, x, block)
                while len(terms) > 1:
                    terms = [terms[t] + terms[t + 1] for t in range(0, len(terms), 2)]
                out = terms[0]
                upper_out[m, r - base : r + BLK - base, :] = jnp.where(lane >= r + sub, out, 0.0)
                right = jnp.where(on_diag, block, out)
                inverse_out[m, r - base : r + BLK - base, :] = jnp.where(lane < r + BLK, right, 0.0)
                if r + BLK < 128:
                    p1, p2, p3 = pieces(right)
                    rhs = jnp.concatenate([p1, p2, p1, p2, p3, p1], axis=0).astype(BF16)
                    lhs = jnp.concatenate([p1, p1, p2, p2, p1, p3], axis=0).astype(BF16)
                    update = jnp.dot(lhs.T[r + BLK :], rhs, preferred_element_type=F32)
                    at = lax.broadcasted_iota(jnp.int32, (128 - r - BLK, 128), 1)
                    old = work[m, r + BLK - base :, :]
                    work[m, r + BLK - base :, :] = jnp.where((at >= r) & (at < r + BLK), 0.0, old) - update


def times_transposed(x, y):
    return lax.dot_general(
        x, y, (((1,), (1,)), ((), ())), precision=lax.Precision.HIGHEST, preferred_element_type=F32
    )


def local_factor_kernel(first, last, g_ref, *refs):
    *left, upper_ref, inverse_ref, work = refs
    work[...] = g_ref[...]
    factor_blocks(work, upper_ref, inverse_ref, [list(range(g_ref.shape[0]))], first, last)
    for out in left:
        out[...] = work[:, BLK * (last - first) :, :]


def local_factors(work, first, last):
    n, rows, _ = work.shape
    done = BLK * (last - first)
    outs = [(n, rows - done, 128)] * (done < rows) + [(n, done, 128)] * 2
    kernel = lambda *refs: local_factor_kernel(first, last, *refs)
    return call(kernel, outs, [pltpu.VMEM(work.shape, F32)], 0, (work,))


def whole(parts, m):
    return jnp.concatenate([p[m] for p in parts], axis=0)


def local_basis_kernel(y_ref, *refs):
    *parts, leaf_ref, base_ref, root_ref = refs
    upper, inverse = parts[: len(parts) // 2], parts[len(parts) // 2 :]
    leaves = y_ref.shape[0]
    for m in range(leaves):
        leaf_ref[m * 256 : m * 256 + 256, :] = times_transposed(y_ref[m], whole(inverse, m))
    for n in range(leaves - 1):
        inner = whole(inverse, leaves + n)
        for half in range(2):
            base_ref[n, half * 128 : half * 128 + 128, :] = times_transposed(whole(upper, 2 * n + half), inner)
    root_ref[...] = whole(upper, 2 * leaves - 2)


def upper_kernel(low_bits, *refs):
    levels = (len(refs) - 6) // 2
    first = refs[0]
    own = refs[1 : 1 + levels]
    partner = refs[1 + levels : 1 + 2 * levels]
    base_ref, root_ref, work, upper, inverse = refs[1 + 2 * levels :]
    place = (lax.axis_index("tx") << low_bits) + lax.axis_index("ty")
    for m in range(levels):
        unpacked(own[m], work, m)
        unpacked(partner[m], work, levels + m)
    factor_blocks(work, upper, inverse, [list(range(levels)), list(range(levels, 2 * levels))])
    for h in range(levels):
        mine = first[...] if h == 0 else upper[h - 1]
        a = times_transposed(mine, inverse[h])
        b = times_transposed(upper[levels + h], inverse[h])
        bit = (place >> h) & 1
        base_ref[h, pl.ds(bit * 128, 128), :] = a
        base_ref[h, pl.ds((1 - bit) * 128, 128), :] = b
    root_ref[...] = upper[levels - 1]


def per_device(points, tree_order, samples, near_leaves, near_counts):
    leaves = near_counts.shape[0]
    both = ("tx", "ty")
    for_after, for_before = edge_blocks(points, tree_order, samples)
    before = passed_along(for_after, both, 1)
    after = passed_along(for_before, both, -1)
    part, ordered = own_samples(near_leaves, near_counts, points, tree_order, samples)
    sampled, work, gram = halo_samples(near_leaves, near_counts, before, after, part, ordered)
    owns, partners = [], []
    low_bits = lax.axis_size("ty").bit_length() - 1
    high_bits = lax.axis_size("tx").bit_length() - 1
    steps = [("ty", m) for m in [1, 2, 4, 15]] + [("tx", m) for m in [1, 2, 6, 8, 24]]
    assert [m.bit_length() for _, m in steps] == [*range(1, low_bits + 1), *range(1, high_bits + 1)]
    cuts = [0, 3, 8, 16]
    uppers, inverses = [], []
    for h, (axis, mask) in enumerate(steps):
        factoring = h + 1 < len(cuts)
        if factoring:
            work, gram = lax.optimization_barrier((work, gram))
        if h == 3:
            sampled, gram = lax.optimization_barrier((sampled, gram))
        partner = exchanged(gram, axis, mask)
        if factoring:
            out = local_factors(work, cuts[h], cuts[h + 1])
            partner, *out = lax.optimization_barrier((partner, *out))
            work, upper, inverse = out if len(out) == 3 else (None, *out)
            uppers.append(upper)
            inverses.append(inverse)
        if h == 3:
            locals_out = call(
                local_basis_kernel,
                [(leaves * 256, 128), (leaves - 1, 256, 128), (128, 128)],
                [],
                0,
                (sampled, *uppers, *inverses),
            )
            partner, leaf_bases, local_bases, local_root = lax.optimization_barrier((partner, *locals_out))
        gram = gram + partner
        owns.append(gram)
        partners.append(partner)
    levels = len(owns)
    upper_bases, root = call(
        lambda *refs: upper_kernel(low_bits, *refs),
        [(levels, 256, 128), (128, 128)],
        [pltpu.VMEM((2 * levels, 128, 128), F32)] * 3,
        0,
        (local_root, *owns, *partners),
    )
    return leaf_bases, local_bases, upper_bases, root


def solution(mesh):
    return jax.shard_map(
        per_device,
        mesh=mesh,
        in_specs=(
            P(None, ("tx", "ty")),
            P(("tx", "ty"), None),
            P(("tx", "ty"), None),
            P(("tx", "ty"), None),
            P(("tx", "ty")),
        ),
        out_specs=(
            P(("tx", "ty"), None),
            P(("tx", "ty"), None, None),
            P(("tx", "ty"), None, None),
            P(),
        ),
        check_vma=False,
    )
```

```python
import jax
import jax.numpy as jnp
from jax import lax
from jax.experimental import pallas as pl
from jax.experimental.pallas import tpu as pltpu
from jax.sharding import PartitionSpec as P

F32 = jnp.float32
BF16 = jnp.bfloat16
HALO = 2
SPREAD = 50.0
LOG2E = 1.4426950408889634
EXTRA = 64
BLK = 8

def pieces(x):
    a=x.astype(BF16).astype(F32); y=x-a
    b=y.astype(BF16).astype(F32)
    return a,b,y-b
def call(kernel, outs, scratch, prefetch, args, specs=None, alias=None):
    vmem = pl.BlockSpec(memory_space=pltpu.VMEM)
    smem = pl.BlockSpec(memory_space=pltpu.SMEM)
    return pl.pallas_call(kernel,
        out_shape=tuple(jax.ShapeDtypeStruct(s, F32) for s in outs),
        in_specs=[smem] * prefetch + (specs or [vmem] * (len(args) - prefetch)),
        out_specs=tuple([vmem] * len(outs)),
        scratch_shapes=scratch, input_output_aliases=alias or {},
        compiler_params=pltpu.CompilerParams(vmem_limit_bytes=56<<20))(*args)

def edge_kernel(first, last, points, order, up, down):
    n = first.shape[0]
    for out, rows, at in ((up, last, order.shape[1] - n), (down, first, 0)):
        out[:n, :] = rows[...]
        for c in range(3):
            for h in range(16):
                out[n + 16 * c + h : n + 16 * c + h + 1, :] = points[c : c + 1, 128 * h : 128 * h + 128]
        for h in range(n // 128):
            out[n + 48 + h : n + 49 + h, :] = order[:, at + 128 * h : at + 128 * h + 128].astype(F32)
        out[n + 48 + n // 128 :, :] = jnp.zeros((16 - n // 128, 128), F32)

def table_of(rows48):
    return jnp.concatenate(pieces(rows48), axis=0).astype(BF16)

def gathered(table, order_row):
    low = order_row & 127
    high = order_row >> 7
    hot = (lax.broadcasted_iota(jnp.int32, (128, 128), 0) == low).astype(F32).astype(BF16)
    r = jnp.dot(table, hot, preferred_element_type=F32)
    r = (r[0:48] + r[48:96]) + r[96:144]
    pick = lax.broadcasted_iota(jnp.int32, (16, 128), 0) == high
    return [jnp.sum(jnp.where(pick, r[16 * c : 16 * c + 16], 0.0), axis=0, keepdims=True) for c in range(3)]

def split_into(parts, w, block):
    high = block.astype(BF16)
    parts[w, :, :128] = high
    parts[w, :, 128:] = (block - high.astype(F32)).astype(BF16)

def spread_rows(points, rows, i):
    t = points[i].T
    for c in range(3):
        rows[i, c] = jnp.broadcast_to(t[:, c : c + 1], (256, 128))

def tile(rows, i, points, parts, w):
    cols = points[w]
    halves = []
    for g in range(2):
        d = None
        for c in range(3):
            e = rows[i, c] - cols[c : c + 1, 128 * g : 128 * g + 128]
            d = e * e if d is None else d + e * e
        halves.append(jnp.exp2(d * (-SPREAD * LOG2E)))
    kernel = jnp.concatenate(halves, axis=1)
    high = kernel.astype(BF16)
    low = (kernel - high.astype(F32)).astype(BF16)
    both = parts[w]
    out = jnp.dot(high, both, preferred_element_type=F32) + jnp.dot(low, both, preferred_element_type=F32)
    return out[:, :128] + out[:, 128:]

def packed(g, out):
    lane = lax.broadcasted_iota(jnp.int32, (1, 128), 1)
    out[0:32, :] = g[0:32]
    out[32:64, :] = jnp.where(lane < 32, pltpu.roll(g[96:128], 32, 1), g[32:64])
    out[64:80, :] = jnp.where(lane < 64, pltpu.roll(g[80:96], 64, 1), g[64:80])


def unpacked(p, out, m):
    out[m, 0:64, :] = p[0:64, :]
    out[m, 64:80, :] = p[64:80, :]
    out[m, 80:96, :] = pltpu.roll(p[64:80, :], 64, 1)
    out[m, 96:128, :] = pltpu.roll(p[32:64, :], 96, 1)


def list_tiles(near, counts, leaf_of, col_of, wanted, start):
    leaves = counts.shape[0]
    def leaf(i, n):
        def one(k, n):
            w = near[i, k]
            leaf_of[n] = i
            col_of[n] = w
            return n + jnp.where(wanted(w), 1, 0).astype(jnp.int32)
        return lax.fori_loop(0, counts[i], one, n)
    n = lax.fori_loop(0, leaves, leaf, start)
    return n

def run_tiles(n, leaf_of, col_of, at, y, spare, rows, points, parts, width=2):
    leaf_of_pad = spare
    for e in range(width):
        leaf_of[n + e] = spare
        col_of[n + e] = at
    def step(s, c):
        ids = [(leaf_of[s * width + e], col_of[s * width + e] - at) for e in range(width)]
        outs = [tile(rows, jnp.minimum(i, spare - 1), points, parts, w) for i, w in ids]
        for (i, _), o in zip(ids, outs):
            y[i] = y[i] + o
        return c
    lax.fori_loop(0, (n + width - 1) // width, step, 0)

def own_kernel(near, counts, raw, order, own, y_ref, p_ref, acc, parts, rows, tab, leaf_of, col_of):
    leaves = counts.shape[0]
    for c in range(3):
        for h in range(16):
            tab[16 * c + h : 16 * c + h + 1, :] = raw[c : c + 1, 128 * h : 128 * h + 128]
    table = table_of(tab[...])
    for h in range(2 * leaves):
        got = gathered(table, order[:, 128 * h : 128 * h + 128])
        for c in range(3):
            p_ref[h // 2, c : c + 1, 128 * (h % 2) : 128 * (h % 2) + 128] = got[c]
    for i in range(leaves):
        split_into(parts, i, own[256 * i : 256 * i + 256, :])
        p_ref[i, 3:8, :] = jnp.zeros((5, 256), F32)
        spread_rows(p_ref, rows, i)
        leaf_of[i] = i
        col_of[i] = HALO + i
        acc[i] = jnp.zeros((256, 128), F32)
    acc[leaves] = jnp.zeros((256, 128), F32)
    n = list_tiles(near, counts, leaf_of, col_of, lambda w: (w >= HALO) & (w < HALO + leaves), leaves)
    run_tiles(n, leaf_of, col_of, HALO, acc, leaves, rows, p_ref, parts)
    y_ref[...] = acc[:leaves]

def halo_kernel(near, counts, before, after, y_in, p_in, y_ref, g_ref, top_ref, acc, parts, rows, points, leaf_of, col_of):
    leaves = counts.shape[0]
    n_edge = HALO * 256
    for side, src in ((0, before), (1, after)):
        table = table_of(src[n_edge : n_edge + 48, :])
        for h in range(2 * HALO):
            got = gathered(table, src[n_edge + 48 + h : n_edge + 49 + h, :].astype(jnp.int32))
            for c in range(3):
                points[side * HALO + h // 2, c : c + 1, 128 * (h % 2) : 128 * (h % 2) + 128] = got[c]
        for w in range(HALO):
            split_into(parts, side * HALO + w, src[256 * w : 256 * w + 256, :])
    for i in range(leaves):
        spread_rows(p_in, rows, i)
        acc[i] = y_in[i]
    acc[leaves] = jnp.zeros((256, 128), F32)
    n = list_tiles(near, counts, leaf_of, col_of, lambda w: (w < HALO) | (w >= HALO + leaves), 0)
    def fix(t, c):
        w = col_of[t]
        col_of[t] = jnp.where(w < HALO, w, w - leaves)
        return c
    lax.fori_loop(0, n, fix, 0)
    run_tiles(n, leaf_of, col_of, 0, acc, leaves, rows, points, parts)
    for i in range(leaves):
        y = acc[i]
        y_ref[i] = y
        b1, b2, b3 = [p.astype(BF16) for p in pieces(y)]
        b12 = jnp.concatenate([b1, b2], axis=1)
        q = jnp.dot(b12.T, b12, preferred_element_type=F32)
        q = (q[:128] + q[128:])
        t = jnp.dot(b1.T, b3, preferred_element_type=F32) + jnp.dot(b3.T, b1, preferred_element_type=F32)
        g_ref[i] = (q[:, :128] + q[:, 128:]) + t
    at, n = 0, leaves
    while n > 1:
        for c in range(n // 2):
            g_ref[at + n + c] = g_ref[at + 2 * c] + g_ref[at + 2 * c + 1]
        at += n
        n //= 2
    packed(g_ref[at], top_ref)

def edge_blocks(points, order, samples):
    n = HALO * 256
    total = samples.shape[0] // n
    specs = [pl.BlockSpec((n, 128), lambda i: (0, 0)), pl.BlockSpec((n, 128), lambda i: (total - 1, 0)),
             pl.BlockSpec(points.shape, lambda i: (0, 0)), pl.BlockSpec(order.shape, lambda i: (0, 0))]
    o = pl.BlockSpec((n + EXTRA, 128), lambda i: (0, 0))
    return pl.pallas_call(edge_kernel, grid=(1,), in_specs=specs, out_specs=(o, o),
        out_shape=(jax.ShapeDtypeStruct((n + EXTRA, 128), F32),) * 2)(samples, samples, points, order)
def own_samples(near, counts, points, order, samples):
    L = counts.shape[0]
    return call(own_kernel, [(L,256,128),(L,8,256)],
        [pltpu.VMEM((L+1,256,128),F32), pltpu.VMEM((L,256,256),BF16), pltpu.VMEM((L,3,256,128),F32), pltpu.VMEM((48,128),F32), pltpu.SMEM((64,),jnp.int32), pltpu.SMEM((64,),jnp.int32)],
        2, (near, counts, points, order, samples))
def halo_samples(near, counts, before, after, y, p):
    L = counts.shape[0]
    return call(halo_kernel, [(L,256,128),(2*L-1,128,128),(80,128)],
        [pltpu.VMEM((L+1,256,128),F32), pltpu.VMEM((2*HALO,256,256),BF16), pltpu.VMEM((L,3,256,128),F32), pltpu.VMEM((2*HALO,8,256),F32), pltpu.SMEM((64,),jnp.int32), pltpu.SMEM((64,),jnp.int32)],
        2, (near, counts, before, after, y, p))


def passed_along(block, axis, distance):
    devices = range(lax.axis_size(axis))
    route = [(i - distance, i) for i in devices if i - distance in devices]
    return lax.ppermute(block, axis, route)


def exchanged(value, axis, mask):
    return lax.ppermute(value, axis, [(i, i ^ mask) for i in range(lax.axis_size(axis))])


def row_of(x, j):
    return jnp.broadcast_to(x[j : j + 1, :], x.shape)


def factor_blocks(work, upper_out, inverse_out, groups, first=0, last=128 // BLK):
    base = BLK * first
    lane = lax.broadcasted_iota(jnp.int32, (BLK, 128), 1)
    sub = lax.broadcasted_iota(jnp.int32, (BLK, 128), 0)
    for k in range(first, last):
        r = BLK * k
        on_diag = (lane >= r) & (lane < r + BLK)
        for group in groups:
            panel = {m: work[m, r - base : r + BLK - base, :] for m in group}
            diag = None
            for s, m in enumerate(group):
                shift = (BLK * s - r) % 128
                x = pltpu.roll(panel[m], shift, 1) if shift else panel[m]
                diag = x if s == 0 else jnp.where((lane >= BLK * s) & (lane < BLK * s + BLK), x, diag)
            cols = [pltpu.roll(diag, 128 - j, 1) if j else diag for j in range(BLK)]
            inv = [jnp.where(sub == j, 1.0, 0.0).astype(F32) for j in range(BLK)]
            scale = jnp.ones((BLK, 128), F32)
            for j in range(BLK):
                below = jnp.where(sub > j, cols[j], 0.0)
                rs = lax.rsqrt(row_of(cols[j], j))
                mult = below * rs
                for q in range(j + 1, BLK):
                    cols[q] = cols[q] - mult * (row_of(cols[q], j) * rs)
                for q in range(j + 1):
                    inv[q] = inv[q] - mult * (row_of(inv[q], j) * rs)
                scale = jnp.where(sub == j, rs, scale)
            inv = [e * scale for e in inv]
            for s, m in enumerate(group):
                block, terms = None, []
                for q in range(BLK):
                    x = jnp.broadcast_to(inv[q][:, BLK * s : BLK * s + 1], (BLK, 128))
                    terms.append(x * row_of(panel[m], q))
                    block = x if q == 0 else jnp.where(lane == r + q, x, block)
                while len(terms) > 1:
                    terms = [terms[t] + terms[t + 1] for t in range(0, len(terms), 2)]
                out = terms[0]
                upper_out[m, r - base : r + BLK - base, :] = jnp.where(lane >= r + sub, out, 0.0)
                right = jnp.where(on_diag, block, out)
                inverse_out[m, r - base : r + BLK - base, :] = jnp.where(lane < r + BLK, right, 0.0)
                if r + BLK < 128:
                    p1, p2, p3 = pieces(right)
                    rhs = jnp.concatenate([p1, p2, p1, p2, p3, p1], axis=0).astype(BF16)
                    lhs = jnp.concatenate([p1, p1, p2, p2, p1, p3], axis=0).astype(BF16)
                    update = jnp.dot(lhs.T[r + BLK :], rhs, preferred_element_type=F32)
                    at = lax.broadcasted_iota(jnp.int32, (128 - r - BLK, 128), 1)
                    old = work[m, r + BLK - base :, :]
                    work[m, r + BLK - base :, :] = jnp.where((at >= r) & (at < r + BLK), 0.0, old) - update


def times_transposed(x, y):
    return lax.dot_general(
        x, y, (((1,), (1,)), ((), ())), precision=lax.Precision.HIGHEST, preferred_element_type=F32
    )


def local_factor_kernel(first, last, g_ref, *refs):
    *left, upper_ref, inverse_ref, work = refs
    work[...] = g_ref[...]
    factor_blocks(work, upper_ref, inverse_ref, [list(range(g_ref.shape[0]))], first, last)
    for out in left:
        out[...] = work[:, BLK * (last - first) :, :]


def local_factors(work, first, last):
    n, rows, _ = work.shape
    done = BLK * (last - first)
    outs = [(n, rows - done, 128)] * (done < rows) + [(n, done, 128)] * 2
    kernel = lambda *refs: local_factor_kernel(first, last, *refs)
    return call(kernel, outs, [pltpu.VMEM(work.shape, F32)], 0, (work,))


def whole(parts, m):
    return jnp.concatenate([p[m] for p in parts], axis=0)


def local_basis_kernel(y_ref, *refs):
    *parts, leaf_ref, base_ref, root_ref = refs
    upper, inverse = parts[: len(parts) // 2], parts[len(parts) // 2 :]
    leaves = y_ref.shape[0]
    for m in range(leaves):
        leaf_ref[m * 256 : m * 256 + 256, :] = times_transposed(y_ref[m], whole(inverse, m))
    for n in range(leaves - 1):
        inner = whole(inverse, leaves + n)
        for half in range(2):
            base_ref[n, half * 128 : half * 128 + 128, :] = times_transposed(whole(upper, 2 * n + half), inner)
    root_ref[...] = whole(upper, 2 * leaves - 2)


def first_factor_kernel(last, *refs):
    *packs, left, upper_ref, inverse_ref, work = refs
    for m, p in enumerate(packs):
        unpacked(p, work, m)
    factor_blocks(work, upper_ref, inverse_ref, [list(range(len(packs)))], 0, last)
    left[...] = work[:, BLK * last :, :]


def first_factors(packs, last):
    n, done = len(packs), BLK * last
    outs = [(n, 128 - done, 128), (n, done, 128), (n, done, 128)]
    kernel = lambda *refs: first_factor_kernel(last, *refs)
    return call(kernel, outs, [pltpu.VMEM((n, 128, 128), F32)], 0, tuple(packs))


def upper_kernel(low_bits, low, high, *refs):
    first, refs = refs[0], refs[1:]
    parts = (len(refs) - 2 * high - 5) // 2
    low_upper, low_inverse = refs[:parts], refs[parts : 2 * parts]
    packs = refs[2 * parts : 2 * parts + 2 * high]
    base_ref, root_ref, work, upper, inverse = refs[2 * parts + 2 * high :]
    place = (lax.axis_index("tx") << low_bits) + lax.axis_index("ty")
    for m, p in enumerate(packs):
        unpacked(p, work, m)
    factor_blocks(work, upper, inverse, [list(range(2 * high))])
    for h in range(low + high):
        if h == 0:
            mine = first[...]
        else:
            mine = whole(low_upper, h - 1) if h <= low else upper[h - 1 - low]
        other = whole(low_upper, low + h) if h < low else upper[high + h - low]
        inner = whole(low_inverse, h) if h < low else inverse[h - low]
        bit = (place >> h) & 1
        base_ref[h, pl.ds(bit * 128, 128), :] = times_transposed(mine, inner)
        base_ref[h, pl.ds((1 - bit) * 128, 128), :] = times_transposed(other, inner)
    root_ref[...] = upper[high - 1]


def per_device(points, tree_order, samples, near_leaves, near_counts):
    leaves = near_counts.shape[0]
    both = ("tx", "ty")
    for_after, for_before = edge_blocks(points, tree_order, samples)
    before = passed_along(for_after, both, 1)
    after = passed_along(for_before, both, -1)
    part, ordered = own_samples(near_leaves, near_counts, points, tree_order, samples)
    sampled, work, gram = halo_samples(near_leaves, near_counts, before, after, part, ordered)
    owns, partners = [], []
    low_bits = lax.axis_size("ty").bit_length() - 1
    high_bits = lax.axis_size("tx").bit_length() - 1
    steps = [("ty", m) for m in [1, 2, 4, 15]] + [("tx", m) for m in [1, 2, 6, 8, 24]]
    assert [m.bit_length() for _, m in steps] == [*range(1, low_bits + 1), *range(1, high_bits + 1)]
    cuts = [0, 3, 8, 16]
    uppers, inverses, low_uppers, low_inverses = [], [], [], []
    for h, (axis, mask) in enumerate(steps):
        factoring = h + 1 < len(cuts)
        if factoring:
            work, gram = lax.optimization_barrier((work, gram))
        if h == 3:
            sampled, gram = lax.optimization_barrier((sampled, gram))
        if h > low_bits + 1:
            low_work, gram = lax.optimization_barrier((low_work, gram))
        partner = exchanged(gram, axis, mask)
        if factoring:
            out = local_factors(work, cuts[h], cuts[h + 1])
            partner, *out = lax.optimization_barrier((partner, *out))
            work, upper, inverse = out if len(out) == 3 else (None, *out)
            uppers.append(upper)
            inverses.append(inverse)
        if h == 3:
            locals_out = call(
                local_basis_kernel,
                [(leaves * 256, 128), (leaves - 1, 256, 128), (128, 128)],
                [],
                0,
                (sampled, *uppers, *inverses),
            )
            partner, leaf_bases, local_bases, local_root = lax.optimization_barrier((partner, *locals_out))
        if h >= low_bits + 1:
            if h == low_bits + 1:
                out = first_factors([*owns[:low_bits], *partners[:low_bits]], 4)
            else:
                out = local_factors(low_work, low_at, low_at + 4)
            low_at = 4 if h == low_bits + 1 else low_at + 4
            partner, *out = lax.optimization_barrier((partner, *out))
            low_work, upper, inverse = out if len(out) == 3 else (None, *out)
            low_uppers.append(upper)
            low_inverses.append(inverse)
        gram = gram + partner
        owns.append(gram)
        partners.append(partner)
    levels = len(owns)
    upper_bases, root = call(
        lambda *refs: upper_kernel(low_bits, low_bits, high_bits, *refs),
        [(levels, 256, 128), (128, 128)],
        [pltpu.VMEM((2 * high_bits, 128, 128), F32)] * 3,
        0,
        (local_root, *low_uppers, *low_inverses, *owns[low_bits:], *partners[low_bits:]),
    )
    return leaf_bases, local_bases, upper_bases, root


def solution(mesh):
    return jax.shard_map(
        per_device,
        mesh=mesh,
        in_specs=(
            P(None, ("tx", "ty")),
            P(("tx", "ty"), None),
            P(("tx", "ty"), None),
            P(("tx", "ty"), None),
            P(("tx", "ty")),
        ),
        out_specs=(
            P(("tx", "ty"), None),
            P(("tx", "ty"), None, None),
            P(("tx", "ty"), None, None),
            P(),
        ),
        check_vma=False,
    )
```
